32 devices in a mesh: pb: 8 (over z, y), ka: 2 (over x), ha: 2 (over core).
Axes of the slice: x: 2, y: 2, z: 4, core: 2. Of those that a mesh axis runs over, the one named last changes fastest.
Arguments:
- queries: bfloat16 [8192, 256], P(('pb', 'ka'), 'ha'), may hold values from -130 to 130
- key_codes: int32 [8192, 256], P(('ka', 'pb'), 'ha'), may hold values from -127 to 127
- value_codes: int32 [8192, 256], P(('ka', 'pb'), 'ha'), may hold values from -127 to 127
- key_scale: float32 [], replicated, may hold values from 0.015 to 0.02
- value_scale: float32 [], replicated, may hold values from 0.01 to 0.02
- out_grad: bfloat16 [8192, 256], P(('pb', 'ka'), 'ha'), may hold values from -256 to 256
Outputs:
- query_grad: float32 [8192, 256], P(('pb', 'ka'), 'ha')
- key_grad: float32 [8192, 256], P(('ka', 'pb'), 'ha')
- value_grad: float32 [8192, 256], P(('ka', 'pb'), 'ha')
The draws below stay inside these ranges and needn't reach their ends.
All inputs are finite; a program needn't handle non-finite values.
Results may differ from the reference program's by a relative error of at most 0.017.
Values may be sent and summed in bfloat16 or wider, within the bound.
A program may use at most 128 MiB of HBM per device.

```python
import math
import jax
import jax.numpy as jnp
import numpy as np
from jax import lax

HD = 128
HEADS = 2
SEQ = 8192


def shared_codes(key):
    base = jax.random.fold_in(key, 11)
    code_key, scale_key = jax.random.split(base)
    raw = jax.random.randint(code_key, (SEQ, HEADS * HD), -127, 128).astype(jnp.int32)
    positions = jnp.arange(SEQ, dtype=jnp.int32)
    limits = 107 + 20 * (positions + 1) // SEQ
    table = raw * limits[:, None] // 127
    table = jnp.clip(table, -127, 127).astype(jnp.int32)
    anchors = np.array([index * SEQ // 8 + SEQ // 16 for index in range(8)])
    lasts = np.array([head * HD + HD - 1 for head in range(HEADS)])
    table = table.at[anchors + 1].set(table[anchors])
    table = table.at[anchors[:, None], lasts[None, :]].set(127)
    table = table.at[anchors[:, None] + 1, lasts[None, :]].set(102)
    table = table.at[SEQ - 1, 0].set(-127)
    factor = jnp.exp(jax.random.uniform(scale_key, (), jnp.float32, math.log(0.015), math.log(0.02)))
    return (table, factor)


def draw_key_codes(key, part):
    return shared_codes(key)[0]


def draw_key_scale(key, part):
    return shared_codes(key)[1]


def draw_queries(key, part):
    result = 2.0 * jax.random.normal(jax.random.fold_in(key, 5), (SEQ, HEADS * HD), jnp.float32)
    return result.astype(jnp.bfloat16)


def set_ends(values, key, low, top_value):
    dims = values.shape
    place = [jax.random.randint(jax.random.fold_in(key, axis), (), 0, dims[axis]) for axis in range(len(dims))]
    values = values.at[tuple(place)].set(low)
    longest = dims.index(max(dims))
    place[longest] = (place[longest] + 1) % dims[longest]
    return values.at[tuple(place)].set(top_value)


def block_scale(own_key, extent, pieces, least, largest):
    def one(axis_at, shards_of):
        heights = jax.random.uniform(jax.random.fold_in(jax.random.fold_in(own_key, 6), axis_at), (shards_of,), jnp.float32, least / len(pieces), largest / len(pieces))
        return jnp.repeat(jnp.exp(heights), extent[axis_at] // shards_of).reshape((-1,) + (1,) * (len(extent) - axis_at - 1))

    gain = one(*pieces[0])
    for cut in pieces[1:]:
        gain = gain * one(*cut)
    return gain


def scatter_about(rng, shape, deviation, limit, cuts=(), held_as=jnp.bfloat16):
    values = jax.random.normal(rng, shape, jnp.float32) * deviation
    if len(cuts) > 0:
        values = block_scale(rng, shape, cuts, -0.22, 0.18) * values
    return jnp.clip(values, min=-limit, max=limit).astype(held_as)


def setup_inputs(seed: int = 0) -> dict:
    streams_of = jax.random.split(jax.random.key(seed), 7)
    queries = draw_queries(jax.random.fold_in(streams_of[6], 71), 0)
    key_codes = draw_key_codes(jax.random.fold_in(streams_of[6], 71), 0)
    value_codes = set_ends(jax.random.randint(streams_of[2], (SEQ, HEADS * HD), -127, 128), jax.random.fold_in(streams_of[2], 1), -127, 127).astype(jnp.int32)
    key_scale = draw_key_scale(jax.random.fold_in(streams_of[6], 71), 0)
    value_scale = jnp.clip(jnp.exp(jax.random.uniform(streams_of[4], (), jnp.float32, math.log(0.01), math.log(0.02))), 0.01, 0.02)
    out_grad = scatter_about(streams_of[5], (SEQ, HEADS * HD), (0.5 * SEQ ** 0.5), 256.0, ((0, 16), (1, 2)))
    return dict(queries=queries, key_codes=key_codes, value_codes=value_codes, key_scale=key_scale, value_scale=value_scale, out_grad=out_grad)


def dequantize(table, factor):
    return (table.astype(jnp.float32) * factor).astype(jnp.bfloat16)

def contract_last(left, right):
    return lax.dot_general(left, right, (((1,), (1,)), ((), ())), preferred_element_type=jnp.float32)

def contract_first(left, right):
    return lax.dot_general(left, right, (((0,), (0,)), ((), ())), preferred_element_type=jnp.float32)

def reference(queries, key_codes, value_codes, key_scale, value_scale, out_grad):
    keys = dequantize(key_codes, key_scale)
    values = dequantize(value_codes, value_scale)
    factor = 1.0 / math.sqrt(HD)
    block_rows = 1024 if SEQ % 1024 == 0 else SEQ
    block_count = SEQ // block_rows
    q_parts, k_parts, v_parts = ([], [], [])
    for head in range(HEADS):
        cols = slice(head * HD, (head + 1) * HD)
        q_head = queries[:, cols].reshape(block_count, block_rows, HD)
        d_head = out_grad[:, cols].reshape(block_count, block_rows, HD)
        k_head = keys[:, cols]
        v_head = values[:, cols]

        def step(totals, inputs):
            k_grad, v_grad = totals
            q_block, d_block = inputs
            scores = contract_last(q_block, k_head) * factor
            row_max = lax.optimization_barrier(jnp.max(scores, axis=1, keepdims=True))
            log_total = row_max + jnp.log(lax.optimization_barrier(jnp.sum(jnp.exp(scores - row_max), axis=1, keepdims=True)))
            probs = jnp.exp(scores - log_total)
            d_probs = contract_last(d_block, v_head)
            row_delta = lax.optimization_barrier(jnp.sum(probs * d_probs, axis=1, keepdims=True))
            d_scores = probs * (d_probs - row_delta)
            probs_low = probs.astype(jnp.bfloat16)
            d_scores_low = d_scores.astype(jnp.bfloat16)
            q_grad = jnp.dot(d_scores_low, k_head, preferred_element_type=jnp.float32) * factor
            k_grad = k_grad + contract_first(d_scores_low, q_block) * factor
            v_grad = v_grad + contract_first(probs_low, d_block)
            return ((k_grad, v_grad), q_grad)
        zeros = jnp.zeros((SEQ, HD), jnp.float32)
        (k_grad, v_grad), q_grad = lax.scan(step, (zeros, zeros), (q_head, d_head))
        q_parts.append(q_grad.reshape(SEQ, HD))
        k_parts.append(k_grad)
        v_parts.append(v_grad)
    return (jnp.concatenate(q_parts, axis=1), jnp.concatenate(k_parts, axis=1), jnp.concatenate(v_parts, axis=1))
```

```python
import functools
import math

import jax
import jax.numpy as jnp
from jax import lax
from jax.experimental import pallas as pl
from jax.experimental.pallas import tpu as pltpu
from jax.sharding import PartitionSpec as P

MESH = pl.DeviceIdType.MESH
LOW = jnp.bfloat16
WIDE = jnp.float32


def flipped(rank, step, count):
    total = 0
    bit = 1
    while bit < count:
        one = (rank // bit) % 2
        two = (step // bit) % 2
        total = total + bit * (one + two - 2 * one * two)
        bit *= 2
    return total


def contract(left, right, dims):
    return lax.dot_general(left, right, ((dims[:1], dims[1:]), ((), ())), preferred_element_type=WIDE)


def kernel(
    nq, nk, nka, fold,
    key_scale, value_scale, q_ref, g_ref, kc_ref, vc_ref,
    dq_ref, dk_ref, dv_ref,
    qd, kv, stats, lse, delta, acc_q, acc_k, acc_v,
    gk_out, gk_in, gq_out, gq_in,
    q_send, q_recv, k_send, k_recv, s_send, s_recv, gk_send, gk_recv, gq_send, gq_recv,
):
    rows, width = q_ref.shape
    factor = 1.0 / math.sqrt(width)
    log2e = math.log2(math.e)
    pb, ka = lax.axis_index("pb"), lax.axis_index("ka")
    my_q = pb // fold
    low = pb % fold
    my_k = low * nka + ka

    def q_peer(rank):
        return {"pb": rank * fold + low, "ka": ka}

    def k_peer(rank):
        return {"pb": my_q * fold + rank // nka, "ka": rank % nka}

    def q_copy(rank, slot):
        return pltpu.make_async_remote_copy(
            qd.at[slot], qd.at[slot], q_send.at[rank], q_recv.at[slot],
            device_id=q_peer(rank), device_id_type=MESH)

    def k_copy(rank, slot):
        return pltpu.make_async_remote_copy(
            kv.at[slot], kv.at[slot], k_send.at[rank], k_recv.at[slot],
            device_id=k_peer(rank), device_id_type=MESH)

    def s_copy(rank, slot):
        return pltpu.make_async_remote_copy(
            stats.at[slot], stats.at[slot], s_send.at[rank], s_recv.at[slot],
            device_id=q_peer(rank), device_id_type=MESH)

    def gk_copy(rank, slot):
        return pltpu.make_async_remote_copy(
            gk_out.at[rank], gk_in.at[slot], gk_send.at[rank], gk_recv.at[slot],
            device_id=k_peer(rank), device_id_type=MESH)

    def gq_copy(rank, slot):
        return pltpu.make_async_remote_copy(
            gq_out.at[rank], gq_in.at[slot], gq_send.at[rank], gq_recv.at[slot],
            device_id=q_peer(rank), device_id_type=MESH)

    barrier = pltpu.get_barrier_semaphore()
    for step in range(1, nq):
        pl.semaphore_signal(barrier, inc=1, device_id=q_peer(flipped(my_q, step, nq)), device_id_type=MESH)
    for step in range(1, nk):
        pl.semaphore_signal(barrier, inc=1, device_id=k_peer(flipped(my_k, step, nk)), device_id_type=MESH)
    qd[my_q, 0] = q_ref[...]
    qd[my_q, 1] = g_ref[...]
    kv[my_k, 0] = (kc_ref[...].astype(WIDE) * key_scale[0]).astype(LOW)
    kv[my_k, 1] = (vc_ref[...].astype(WIDE) * value_scale[0]).astype(LOW)
    pl.semaphore_wait(barrier, nq + nk - 2)

    for step in range(1, nq):
        q_copy(flipped(my_q, step, nq), my_q).start()
    for step in range(1, nk):
        k_copy(flipped(my_k, step, nk), my_k).start()

    @pl.loop(0, nq)
    def _(jj):
        j = flipped(my_q, jj, nq)

        @pl.when(jj > 0)
        def _():
            q_copy(j, j).wait_recv()

        def step_keys(ii, state):
            top, total, dot = state
            i = flipped(my_k, ii, nk)

            @pl.when((jj == 0) & (ii > 0))
            def _():
                k_copy(i, i).wait_recv()

            scores = contract(kv[i, 0], qd[j, 0], (1, 1)) * (factor * log2e)
            d_probs = contract(kv[i, 1], qd[j, 1], (1, 1))
            new_top = jnp.maximum(top, jnp.max(scores, axis=0, keepdims=True))
            shifted = jnp.exp2(scores - new_top)
            old = jnp.exp2(top - new_top)
            total = total * old + jnp.sum(shifted, axis=0, keepdims=True)
            dot = dot * old + jnp.sum(shifted * d_probs, axis=0, keepdims=True)
            return new_top, total, dot

        zero = jnp.zeros((1, rows), WIDE)
        top, total, dot = lax.fori_loop(0, nk, step_keys, (zero - 1e30, zero, zero))
        stats[my_q, pl.ds(j, 1), :] = top + jnp.log2(total)
        stats[my_q, pl.ds(nq + j, 1), :] = dot / total

    for step in range(1, nq):
        s_copy(flipped(my_q, step, nq), my_q).start()
    for step in range(1, nq):
        other = flipped(my_q, step, nq)
        s_copy(other, other).wait_recv()
    parts = [stats[r, 0:nq, :] for r in range(nq)]
    best = functools.reduce(jnp.maximum, parts)
    weights = [jnp.exp2(part - best) for part in parts]
    whole = sum(weights)
    lse[...] = best + jnp.log2(whole)
    delta[...] = sum(w * stats[r, nq : 2 * nq, :] for r, w in enumerate(weights)) / whole

    acc_q[...] = jnp.zeros_like(acc_q)

    @pl.loop(1, nk + 1)
    def _(ii):
        i = flipped(my_k, ii % nk, nk)
        acc_k[...] = jnp.zeros_like(acc_k)
        acc_v[...] = jnp.zeros_like(acc_v)

        @pl.loop(1, nq + 1)
        def _(jj):
            j = flipped(my_q, jj % nq, nq)
            keys, queries, grads = kv[i, 0], qd[j, 0], qd[j, 1]
            scores = contract(keys, queries, (1, 1)) * (factor * log2e)
            d_probs = contract(kv[i, 1], grads, (1, 1))
            probs = jnp.exp2(scores - lse[pl.ds(j, 1), :])
            d_scores = (probs * (d_probs - delta[pl.ds(j, 1), :])).astype(LOW)
            acc_v[...] += contract(probs.astype(LOW), grads, (1, 0))
            acc_k[...] += contract(d_scores, queries, (1, 0))
            acc_q[j] += contract(d_scores, keys, (0, 0))

            @pl.when((ii == nk) & (jj < nq))
            def _():
                gq_out[j] = (acc_q[j] * factor).astype(LOW)
                gq_copy(j, my_q).start()

        @pl.when(ii < nk)
        def _():
            gk_out[i, 0] = (acc_k[...] * factor).astype(LOW)
            gk_out[i, 1] = acc_v[...].astype(LOW)
            gk_copy(i, my_k).start()

    key_sum, value_sum = acc_k[...] * factor, acc_v[...]
    for step in range(1, nk):
        other = flipped(my_k, step, nk)
        gk_copy(other, other).wait_recv()
        key_sum = key_sum + gk_in[other, 0].astype(WIDE)
        value_sum = value_sum + gk_in[other, 1].astype(WIDE)
    dk_ref[...] = key_sum
    dv_ref[...] = value_sum
    query_sum = acc_q[my_q] * factor
    for step in range(1, nq):
        other = flipped(my_q, step, nq)
        gq_copy(other, other).wait_recv()
        query_sum = query_sum + gq_in[other].astype(WIDE)
    dq_ref[...] = query_sum
    for step in range(1, nq):
        other = flipped(my_q, step, nq)
        q_copy(other, my_q).wait_send()
        s_copy(other, my_q).wait_send()
        gq_copy(other, my_q).wait_send()
    for step in range(1, nk):
        other = flipped(my_k, step, nk)
        k_copy(other, my_k).wait_send()
        gk_copy(other, my_k).wait_send()


def shards(queries, key_codes, value_codes, key_scale, value_scale, out_grad):
    rows, width = queries.shape
    npb, nka = lax.axis_size("pb"), lax.axis_size("ka")
    fold = 2
    nq, nk = npb // fold, fold * nka
    vmem = pl.BlockSpec(memory_space=pltpu.VMEM)
    smem = pl.BlockSpec(memory_space=pltpu.SMEM)
    out = jax.ShapeDtypeStruct((rows, width), WIDE)
    sems = [pltpu.SemaphoreType.DMA((n,)) for n in (nq, nq, nk, nk, nq, nq, nk, nk, nq, nq)]
    return tuple(
        pl.pallas_call(
            functools.partial(kernel, nq, nk, nka, fold),
            out_shape=(out, out, out),
            in_specs=[smem, smem, vmem, vmem, vmem, vmem],
            out_specs=(vmem, vmem, vmem),
            scratch_shapes=[
                pltpu.VMEM((nq, 2, rows, width), LOW),
                pltpu.VMEM((nk, 2, rows, width), LOW),
                pltpu.VMEM((nq, 2 * nq, rows), WIDE),
                pltpu.VMEM((nq, rows), WIDE),
                pltpu.VMEM((nq, rows), WIDE),
                pltpu.VMEM((nq, rows, width), WIDE),
                pltpu.VMEM((rows, width), WIDE),
                pltpu.VMEM((rows, width), WIDE),
                pltpu.VMEM((nk, 2, rows, width), LOW),
                pltpu.VMEM((nk, 2, rows, width), LOW),
                pltpu.VMEM((nq, rows, width), LOW),
                pltpu.VMEM((nq, rows, width), LOW),
                *sems,
            ],
            compiler_params=pltpu.CompilerParams(
                collective_id=0, has_side_effects=True, vmem_limit_bytes=48 << 20
            ),
        )(key_scale.reshape(1), value_scale.reshape(1), queries, out_grad, key_codes, value_codes)
    )


def solution(mesh):
    in_specs = (
        P(("pb", "ka"), "ha"),
        P(("ka", "pb"), "ha"),
        P(("ka", "pb"), "ha"),
        P(),
        P(),
        P(("pb", "ka"), "ha"),
    )
    out_specs = (P(("pb", "ka"), "ha"), P(("ka", "pb"), "ha"), P(("ka", "pb"), "ha"))
    return jax.shard_map(shards, mesh=mesh, in_specs=in_specs, out_specs=out_specs, check_vma=False)
```

```python
import functools
import math

import jax
import jax.numpy as jnp
from jax import lax
from jax.experimental import pallas as pl
from jax.experimental.pallas import tpu as pltpu
from jax.sharding import PartitionSpec as P

MESH = pl.DeviceIdType.MESH
LOW = jnp.bfloat16
WIDE = jnp.float32


def flipped(rank, step, count):
    total = 0
    bit = 1
    while bit < count:
        one = (rank // bit) % 2
        two = (step // bit) % 2
        total = total + bit * (one + two - 2 * one * two)
        bit *= 2
    return total


def contract(left, right, dims):
    return lax.dot_general(left, right, ((dims[:1], dims[1:]), ((), ())), preferred_element_type=WIDE)


def kernel(
    nq, nk, nka,
    key_scale, value_scale, q_ref, g_ref, kc_ref, vc_ref,
    dq_ref, dk_ref, dv_ref,
    qd, kv, codes, top, total, dot, stats, lse, delta, acc_q, acc_k, acc_v,
    gk_out, gk_in, gq_out, gq_in,
    load, q_send, q_recv, k_send, k_recv, s_send, s_recv, gk_send, gk_recv, gq_send, gq_recv,
):
    rows, width = q_ref.shape
    factor = 1.0 / math.sqrt(width)
    log2e = math.log2(math.e)
    pb, ka = lax.axis_index("pb"), lax.axis_index("ka")
    my_a, my_k = pb // nk, pb % nk
    my_q = my_a * nka + ka

    def q_rank(step):
        return flipped(my_q, step, nq)

    def k_rank(step):
        return flipped(my_k, step, nk)

    def q_peer(rank):
        return {"pb": (rank // nka) * nk + my_k, "ka": rank % nka}

    def k_peer(rank):
        return {"pb": my_a * nk + rank, "ka": ka}

    def q_copy(block, part, to, sem):
        b, t, s = q_rank(block), q_rank(to), q_rank(sem)
        return pltpu.make_async_remote_copy(
            qd.at[b, part], qd.at[b, part], q_send.at[s, part], q_recv.at[b, part],
            device_id=q_peer(t), device_id_type=MESH)

    def k_copy(block, part, to, sem):
        b, t, s = k_rank(block), k_rank(to), k_rank(sem)
        return pltpu.make_async_remote_copy(
            kv.at[b, part], kv.at[b, part], k_send.at[s, part], k_recv.at[b, part],
            device_id=k_peer(t), device_id_type=MESH)

    def s_copy(rank, slot):
        return pltpu.make_async_remote_copy(
            stats.at[slot], stats.at[slot], s_send.at[rank], s_recv.at[slot],
            device_id=q_peer(rank), device_id_type=MESH)

    def gk_copy(rank, slot):
        return pltpu.make_async_remote_copy(
            gk_out.at[rank], gk_in.at[slot], gk_send.at[rank], gk_recv.at[slot],
            device_id=k_peer(rank), device_id_type=MESH)

    def gq_copy(rank, slot):
        return pltpu.make_async_remote_copy(
            gq_out.at[rank], gq_in.at[slot], gq_send.at[rank], gq_recv.at[slot],
            device_id=q_peer(rank), device_id_type=MESH)

    loads = [
        pltpu.make_async_copy(q_ref, qd.at[my_q, 0], load.at[0]),
        pltpu.make_async_copy(g_ref, qd.at[my_q, 1], load.at[1]),
        pltpu.make_async_copy(kc_ref, codes.at[0], load.at[2]),
        pltpu.make_async_copy(vc_ref, codes.at[1], load.at[3]),
    ]
    for one in loads:
        one.start()
    barrier = pltpu.get_barrier_semaphore()
    for step in range(1, nq):
        pl.semaphore_signal(barrier, inc=1, device_id=q_peer(q_rank(step)), device_id_type=MESH)
    for step in range(1, nk):
        pl.semaphore_signal(barrier, inc=1, device_id=k_peer(k_rank(step)), device_id_type=MESH)
    for one in loads:
        one.wait()
    kv[my_k, 0] = (codes[0].astype(WIDE) * key_scale[0]).astype(LOW)
    kv[my_k, 1] = (codes[1].astype(WIDE) * value_scale[0]).astype(LOW)
    pl.semaphore_wait(barrier, nq + nk - 2)

    for part in range(2):
        q_copy(0, part, nka, nka).start()
        for step in range(2, nk, 2):
            k_copy(0, part, step, step).start()
        k_copy(0, part, 1, 1).start()
        for step in range(1, nka):
            q_copy(0, part, step, step).start()
    top[...] = jnp.full_like(top, -1e30)
    total[...] = jnp.zeros_like(total)
    dot[...] = jnp.zeros_like(dot)
    acc_q[...] = jnp.zeros_like(acc_q)
    acc_k[...] = jnp.zeros_like(acc_k)
    acc_v[...] = jnp.zeros_like(acc_v)

    def first(jj, ii):
        j, i = q_rank(jj), k_rank(ii)
        row = pl.ds(j, 1)
        scores = contract(kv[i, 0], qd[j, 0], (1, 1)) * (factor * log2e)
        d_probs = contract(kv[i, 1], qd[j, 1], (1, 1))
        old_top = top[row, :]
        new_top = jnp.maximum(old_top, jnp.max(scores, axis=0, keepdims=True))
        shifted = jnp.exp2(scores - new_top)
        old = jnp.exp2(old_top - new_top)
        total[row, :] = total[row, :] * old + jnp.sum(shifted, axis=0, keepdims=True)
        dot[row, :] = dot[row, :] * old + jnp.sum(shifted * d_probs, axis=0, keepdims=True)
        top[row, :] = new_top

    def first_over(j_range, i_range):
        if len(j_range) * len(i_range) == 0:
            return

        @pl.loop(0, len(j_range) * len(i_range))
        def _(n):
            first(
                j_range.start + n // len(i_range) * j_range.step,
                i_range.start + n % len(i_range) * i_range.step,
            )

    first_over(range(0, 1), range(0, 1))
    for part in range(2):
        k_copy(1, part, 1, 1).wait_recv()
    first_over(range(0, 1), range(1, 2))
    for step in range(1, nka):
        for part in range(2):
            q_copy(step, part, step, step).wait_recv()
    first_over(range(1, nka), range(0, 2))
    for part in range(2):
        q_copy(nka, part, nka, nka).wait_recv()
        for step in range(1, nka):
            q_copy(nka, part, step, nka + step).start()
        for step in range(2, nk, 2):
            k_copy(step, part, step, step).wait_recv()
            k_copy(step, part, 1, step + 1).start()
    first_over(range(0, nka + 1), range(2, nk, 2))
    first_over(range(nka, nka + 1), range(0, 2))
    for step in range(3, nk, 2):
        for part in range(2):
            k_copy(step, part, step, step).wait_recv()
    first_over(range(0, nka + 1), range(3, nk, 2))
    for step in range(nka + 1, nq):
        for part in range(2):
            q_copy(step, part, step, step).wait_recv()
    first_over(range(nka + 1, nq), range(0, nk))

    stats[my_q, 0:nq, :] = top[...] + jnp.log2(total[...])
    stats[my_q, nq : 2 * nq, :] = dot[...] / total[...]
    for step in range(1, nq):
        s_copy(q_rank(nq - step), my_q).start()
    for step in range(1, nq):
        other = q_rank(step)
        s_copy(other, other).wait_recv()
    parts = [stats[r, 0:nq, :] for r in range(nq)]
    best = functools.reduce(jnp.maximum, parts)
    weights = [jnp.exp2(part - best) for part in parts]
    whole = sum(weights)
    lse[...] = best + jnp.log2(whole)
    delta[...] = sum(w * stats[r, nq : 2 * nq, :] for r, w in enumerate(weights)) / whole

    def second(jj, ii):
        j, i = q_rank(jj), k_rank(ii)
        keys, queries, grads = kv[i, 0], qd[j, 0], qd[j, 1]
        scores = contract(keys, queries, (1, 1)) * (factor * log2e)
        d_probs = contract(kv[i, 1], grads, (1, 1))
        probs = jnp.exp2(scores - lse[pl.ds(j, 1), :])
        d_scores = (probs * (d_probs - delta[pl.ds(j, 1), :])).astype(LOW)
        acc_v[i] += contract(probs.astype(LOW), grads, (1, 0))
        acc_k[i] += contract(d_scores, queries, (1, 0))
        acc_q[j] += contract(d_scores, keys, (0, 0))

    def send_keys(ii):
        i = k_rank(ii)
        gk_out[i, 0] = (acc_k[i] * factor).astype(LOW)
        gk_out[i, 1] = acc_v[i].astype(LOW)
        gk_copy(i, my_k).start()

    def send_queries(jj):
        j = q_rank(jj)
        gq_out[j] = (acc_q[j] * factor).astype(LOW)
        gq_copy(j, my_q).start()

    @pl.loop(0, nk - 2)
    def _(n):
        ii = nk - 1 - n

        @pl.loop(0, nq)
        def _(jj):
            second(jj, ii)

        send_keys(ii)

    @pl.loop(0, nq - nka)
    def _(n):
        jj = nq - 1 - n

        @pl.loop(0, 2)
        def _(m):
            second(jj, 1 - m)

        send_queries(jj)

    @pl.loop(0, 2 * nka)
    def _(n):
        jj = nka - 1 - n % nka
        second(jj, 1 - n // nka)

        @pl.when(n == nka - 1)
        def _():
            send_keys(1)

        @pl.when((n >= nka) & (jj > 0))
        def _():
            send_queries(jj)

    key_sum, value_sum = acc_k[my_k] * factor, acc_v[my_k]
    for step in range(nk - 1, 0, -1):
        other = k_rank(step)
        gk_copy(other, other).wait_recv()
        key_sum = key_sum + gk_in[other, 0].astype(WIDE)
        value_sum = value_sum + gk_in[other, 1].astype(WIDE)
    dk_ref[...] = key_sum
    dv_ref[...] = value_sum
    query_sum = acc_q[my_q] * factor
    for step in range(nq - 1, 0, -1):
        other = q_rank(step)
        gq_copy(other, other).wait_recv()
        query_sum = query_sum + gq_in[other].astype(WIDE)
    dq_ref[...] = query_sum
    for step in range(1, nq):
        other = q_rank(step)
        for part in range(2):
            q_copy(0, part, step, step).wait_send()
        s_copy(other, my_q).wait_send()
        gq_copy(other, my_q).wait_send()
    for step in range(1, nk):
        other = k_rank(step)
        for part in range(2):
            k_copy(0, part, step, step).wait_send()
        gk_copy(other, my_k).wait_send()


def shards(queries, key_codes, value_codes, key_scale, value_scale, out_grad):
    rows, width = queries.shape
    npb, nka = lax.axis_size("pb"), lax.axis_size("ka")
    nq, nk = 2 * nka, npb // 2
    vmem = pl.BlockSpec(memory_space=pltpu.VMEM)
    hbm = pl.BlockSpec(memory_space=pltpu.HBM)
    smem = pl.BlockSpec(memory_space=pltpu.SMEM)
    out = jax.ShapeDtypeStruct((rows, width), WIDE)
    counts = ((4,), (nq, 2), (nq, 2), (nk, 2), (nk, 2), (nq,), (nq,), (nk,), (nk,), (nq,), (nq,))
    sems = [pltpu.SemaphoreType.DMA(count) for count in counts]
    return tuple(
        pl.pallas_call(
            functools.partial(kernel, nq, nk, nka),
            out_shape=(out, out, out),
            in_specs=[smem, smem, hbm, hbm, hbm, hbm],
            out_specs=(vmem, vmem, vmem),
            scratch_shapes=[
                pltpu.VMEM((nq, 2, rows, width), LOW),
                pltpu.VMEM((nk, 2, rows, width), LOW),
                pltpu.VMEM((2, rows, width), jnp.int32),
                pltpu.VMEM((nq, rows), WIDE),
                pltpu.VMEM((nq, rows), WIDE),
                pltpu.VMEM((nq, rows), WIDE),
                pltpu.VMEM((nq, 2 * nq, rows), WIDE),
                pltpu.VMEM((nq, rows), WIDE),
                pltpu.VMEM((nq, rows), WIDE),
                pltpu.VMEM((nq, rows, width), WIDE),
                pltpu.VMEM((nk, rows, width), WIDE),
                pltpu.VMEM((nk, rows, width), WIDE),
                pltpu.VMEM((nk, 2, rows, width), LOW),
                pltpu.VMEM((nk, 2, rows, width), LOW),
                pltpu.VMEM((nq, rows, width), LOW),
                pltpu.VMEM((nq, rows, width), LOW),
                *sems,
            ],
            compiler_params=pltpu.CompilerParams(
                collective_id=0, has_side_effects=True, vmem_limit_bytes=60 << 20
            ),
        )(key_scale.reshape(1), value_scale.reshape(1), queries, out_grad, key_codes, value_codes)
    )


def solution(mesh):
    in_specs = (
        P(("pb", "ka"), "ha"),
        P(("ka", "pb"), "ha"),
        P(("ka", "pb"), "ha"),
        P(),
        P(),
        P(("pb", "ka"), "ha"),
    )
    out_specs = (P(("pb", "ka"), "ha"), P(("ka", "pb"), "ha"), P(("ka", "pb"), "ha"))
    return jax.shard_map(shards, mesh=mesh, in_specs=in_specs, out_specs=out_specs, check_vma=False)
```

```python
import functools
import math

import jax
import jax.numpy as jnp
from jax import lax
from jax.experimental import pallas as pl
from jax.experimental.pallas import tpu as pltpu
from jax.sharding import PartitionSpec as P

MESH = pl.DeviceIdType.MESH
LOW = jnp.bfloat16
PARTS = 4
WIDE = jnp.float32


def flipped(rank, step, count):
    total = 0
    bit = 1
    while bit < count:
        one = (rank // bit) % 2
        two = (step // bit) % 2
        total = total + bit * (one + two - 2 * one * two)
        bit *= 2
    return total


def contract(left, right, dims):
    return lax.dot_general(left, right, ((dims[:1], dims[1:]), ((), ())), preferred_element_type=WIDE)


def kernel(
    nq, nk, nka,
    key_scale, value_scale, q_ref, g_ref, kc_ref, vc_ref,
    dq_ref, dk_ref, dv_ref,
    qd, kv, codes, top, total, dot, stats, lse, delta, acc_q, acc_k, acc_v,
    gk_out, gk_mid, gk_in, gq_out, gq_mid, gq_in,
    load, q_send, q_recv, k_send, k_recv, s_send, s_recv,
    gk_send, gk_mid_recv, gk_recv, gq_send, gq_mid_recv, gq_recv,
):
    rows, width = q_ref.shape
    factor = 1.0 / math.sqrt(width)
    log2e = math.log2(math.e)
    pb, ka = lax.axis_index("pb"), lax.axis_index("ka")
    my_a, my_k = pb // nk, pb % nk
    my_q = my_a * nka + ka

    def q_rank(step):
        return flipped(my_q, step, nq)

    def k_rank(step):
        return flipped(my_k, step, nk)

    def q_peer(rank):
        return {"pb": (rank // nka) * nk + my_k, "ka": rank % nka}

    def k_peer(rank):
        return {"pb": my_a * nk + rank, "ka": ka}

    def span(part):
        return pl.ds(part % 2 * (rows // 2), rows // 2)

    def q_copy(block, part, to, sem):
        b, t, s = q_rank(block), q_rank(to), q_rank(sem)
        return pltpu.make_async_remote_copy(
            qd.at[b, part // 2, span(part)], qd.at[b, part // 2, span(part)],
            q_send.at[s, part], q_recv.at[b, part],
            device_id=q_peer(t), device_id_type=MESH)

    def k_copy(block, part, to, sem):
        b, t, s = k_rank(block), k_rank(to), k_rank(sem)
        return pltpu.make_async_remote_copy(
            kv.at[b, part // 2, span(part)], kv.at[b, part // 2, span(part)],
            k_send.at[s, part], k_recv.at[b, part],
            device_id=k_peer(t), device_id_type=MESH)

    def s_copy(rank, slot):
        return pltpu.make_async_remote_copy(
            stats.at[slot], stats.at[slot], s_send.at[rank], s_recv.at[slot],
            device_id=q_peer(rank), device_id_type=MESH)

    def gk_copy(rank, slot):
        return pltpu.make_async_remote_copy(
            gk_out.at[rank], gk_in.at[slot], gk_send.at[rank], gk_recv.at[slot],
            device_id=k_peer(rank), device_id_type=MESH)

    def gk_mid_copy(rank):
        return pltpu.make_async_remote_copy(
            gk_out.at[rank], gk_mid.at[rank], gk_send.at[rank], gk_mid_recv.at[rank],
            device_id=k_peer(k_rank(1)), device_id_type=MESH)

    def gq_copy(rank, slot):
        return pltpu.make_async_remote_copy(
            gq_out.at[rank], gq_in.at[slot], gq_send.at[rank], gq_recv.at[slot],
            device_id=q_peer(rank), device_id_type=MESH)

    def gq_mid_copy(step, slot):
        return pltpu.make_async_remote_copy(
            gq_out.at[q_rank(step)], gq_mid.at[slot], gq_send.at[q_rank(step)], gq_mid_recv.at[slot],
            device_id=q_peer(q_rank(step - nka)), device_id_type=MESH)

    loads = [
        pltpu.make_async_copy(q_ref, qd.at[my_q, 0], load.at[0]),
        pltpu.make_async_copy(g_ref, qd.at[my_q, 1], load.at[1]),
        pltpu.make_async_copy(kc_ref, codes.at[0], load.at[2]),
        pltpu.make_async_copy(vc_ref, codes.at[1], load.at[3]),
    ]
    for one in loads:
        one.start()
    barrier = pltpu.get_barrier_semaphore()
    for step in range(1, nq):
        pl.semaphore_signal(barrier, inc=1, device_id=q_peer(q_rank(step)), device_id_type=MESH)
    for step in range(1, nk):
        pl.semaphore_signal(barrier, inc=1, device_id=k_peer(k_rank(step)), device_id_type=MESH)
    for one in loads:
        one.wait()
    kv[my_k, 0] = (codes[0].astype(WIDE) * key_scale[0]).astype(LOW)
    kv[my_k, 1] = (codes[1].astype(WIDE) * value_scale[0]).astype(LOW)
    pl.semaphore_wait(barrier, nq + nk - 2)

    for part in range(PARTS):
        q_copy(0, part, nka, nka).start()
        for step in range(2, nk, 2):
            k_copy(0, part, step, step).start()
        k_copy(0, part, 1, 1).start()
        for step in range(1, nka):
            q_copy(0, part, step, step).start()
    top[...] = jnp.full_like(top, -1e30)
    total[...] = jnp.zeros_like(total)
    dot[...] = jnp.zeros_like(dot)
    acc_q[...] = jnp.zeros_like(acc_q)
    acc_k[...] = jnp.zeros_like(acc_k)
    acc_v[...] = jnp.zeros_like(acc_v)

    def first(jj, ii):
        j, i = q_rank(jj), k_rank(ii)
        row = pl.ds(j, 1)
        scores = contract(kv[i, 0], qd[j, 0], (1, 1)) * (factor * log2e)
        d_probs = contract(kv[i, 1], qd[j, 1], (1, 1))
        old_top = top[row, :]
        new_top = jnp.maximum(old_top, jnp.max(scores, axis=0, keepdims=True))
        shifted = jnp.exp2(scores - new_top)
        old = jnp.exp2(old_top - new_top)
        total[row, :] = total[row, :] * old + jnp.sum(shifted, axis=0, keepdims=True)
        dot[row, :] = dot[row, :] * old + jnp.sum(shifted * d_probs, axis=0, keepdims=True)
        top[row, :] = new_top

    def first_over(j_range, i_range):
        if len(j_range) * len(i_range) == 0:
            return

        @pl.loop(0, len(j_range) * len(i_range))
        def _(n):
            first(
                j_range.start + n // len(i_range) * j_range.step,
                i_range.start + n % len(i_range) * i_range.step,
            )

    def forward(part):
        q_copy(nka, part, nka, nka).wait_recv()
        for step in range(1, nka):
            q_copy(nka, part, step, nka + step).start()
        for step in range(2, nk, 2):
            k_copy(step, part, step, step).wait_recv()
            k_copy(step, part, 1, step + 1).start()

    first_over(range(0, 1), range(0, 1))
    forward(0)
    for part in range(PARTS):
        k_copy(1, part, 1, 1).wait_recv()
    first_over(range(0, 1), range(1, 2))
    forward(1)
    for step in range(1, nka):
        for part in range(PARTS):
            q_copy(step, part, step, step).wait_recv()
    first_over(range(1, nka), range(0, 2))
    for part in range(2, PARTS):
        forward(part)
    first_over(range(0, nka + 1), range(2, nk, 2))
    first_over(range(nka, nka + 1), range(0, 2))
    for step in range(3, nk, 2):
        for part in range(PARTS):
            k_copy(step, part, step, step).wait_recv()
    first_over(range(0, nka + 1), range(3, nk, 2))
    for step in range(nka + 1, nq):
        for part in range(PARTS):
            q_copy(step, part, step, step).wait_recv()
    first_over(range(nka + 1, nq), range(0, nk))

    stats[my_q, 0:nq, :] = top[...] + jnp.log2(total[...])
    stats[my_q, nq : 2 * nq, :] = dot[...] / total[...]
    for step in range(1, nq):
        s_copy(q_rank(nq - step), my_q).start()
    for step in range(1, nq):
        other = q_rank(step)
        s_copy(other, other).wait_recv()
    parts = [stats[r, 0:nq, :] for r in range(nq)]
    best = functools.reduce(jnp.maximum, parts)
    weights = [jnp.exp2(part - best) for part in parts]
    whole = sum(weights)
    lse[...] = best + jnp.log2(whole)
    delta[...] = sum(w * stats[r, nq : 2 * nq, :] for r, w in enumerate(weights)) / whole

    def second(jj, ii):
        j, i = q_rank(jj), k_rank(ii)
        keys, queries, grads = kv[i, 0], qd[j, 0], qd[j, 1]
        scores = contract(keys, queries, (1, 1)) * (factor * log2e)
        d_probs = contract(kv[i, 1], grads, (1, 1))
        probs = jnp.exp2(scores - lse[pl.ds(j, 1), :])
        d_scores = (probs * (d_probs - delta[pl.ds(j, 1), :])).astype(LOW)
        acc_v[i] += contract(probs.astype(LOW), grads, (1, 0))
        acc_k[i] += contract(d_scores, queries, (1, 0))
        acc_q[j] += contract(d_scores, keys, (0, 0))

    def pack_keys(i):
        gk_out[i, 0] = (acc_k[i] * factor).astype(LOW)
        gk_out[i, 1] = acc_v[i].astype(LOW)

    def pack_queries(j):
        gq_out[j] = (acc_q[j] * factor).astype(LOW)

    @pl.loop(0, nk // 2 - 1)
    def _(n):
        ii = nk - 1 - 2 * n

        @pl.loop(0, nq)
        def _(jj):
            second(jj, ii)

        pack_keys(k_rank(ii))
        gk_mid_copy(k_rank(ii)).start()

    @pl.loop(0, nq - nka)
    def _(n):
        jj = nq - 1 - n

        @pl.loop(0, nk // 2 + 1)
        def _(m):
            second(jj, 2 * (m - 1) + 3 * ((nk // 2 + 1 - m) // (nk // 2 + 1)))

        @pl.when(jj > nka)
        def _():
            pack_queries(q_rank(jj))
            gq_mid_copy(jj, my_q).start()

    far = q_rank(nka)
    query_sum = acc_q[far] * factor
    for step in range(1, nka):
        gq_mid_copy(nka + step, q_rank(step)).wait_recv()
        query_sum = query_sum + gq_mid[q_rank(step)].astype(WIDE)
    gq_out[far] = query_sum.astype(LOW)
    gq_copy(far, my_q).start()

    @pl.loop(0, nk // 2 - 1)
    def _(n):
        i = k_rank(2 + 2 * n)

        @pl.loop(0, nka)
        def _(jj):
            second(jj, 2 + 2 * n)

        gk_mid_copy(i).wait_recv()
        gk_out[i, 0] = (acc_k[i] * factor + gk_mid[i, 0].astype(WIDE)).astype(LOW)
        gk_out[i, 1] = (acc_v[i] + gk_mid[i, 1].astype(WIDE)).astype(LOW)
        gk_copy(i, my_k).start()

    @pl.loop(0, 2 * nka)
    def _(n):
        jj = nka - 1 - n % nka
        second(jj, 1 - n // nka)

        @pl.when(n == nka - 1)
        def _():
            pack_keys(k_rank(1))
            gk_copy(k_rank(1), my_k).start()

        @pl.when((n >= nka) & (jj > 0))
        def _():
            pack_queries(q_rank(jj))
            gq_copy(q_rank(jj), my_q).start()

    query_sum = acc_q[my_q] * factor
    for step in range(nka, 0, -1):
        other = q_rank(step)
        gq_copy(other, other).wait_recv()
        query_sum = query_sum + gq_in[other].astype(WIDE)
    dq_ref[...] = query_sum
    key_sum, value_sum = acc_k[my_k] * factor, acc_v[my_k]
    for step in (*range(2, nk, 2), 1):
        other = k_rank(step)
        gk_copy(other, other).wait_recv()
        key_sum = key_sum + gk_in[other, 0].astype(WIDE)
        value_sum = value_sum + gk_in[other, 1].astype(WIDE)
    dk_ref[...] = key_sum
    dv_ref[...] = value_sum
    for step in range(1, nq):
        other = q_rank(step)
        for part in range(PARTS):
            q_copy(0, part, step, step).wait_send()
        s_copy(other, my_q).wait_send()
        gq_copy(other, my_q).wait_send()
    for step in range(1, nk):
        other = k_rank(step)
        for part in range(PARTS):
            k_copy(0, part, step, step).wait_send()
        gk_copy(other, my_k).wait_send()


def shards(queries, key_codes, value_codes, key_scale, value_scale, out_grad):
    rows, width = queries.shape
    npb, nka = lax.axis_size("pb"), lax.axis_size("ka")
    nq, nk = 2 * nka, npb // 2
    vmem = pl.BlockSpec(memory_space=pltpu.VMEM)
    hbm = pl.BlockSpec(memory_space=pltpu.HBM)
    smem = pl.BlockSpec(memory_space=pltpu.SMEM)
    out = jax.ShapeDtypeStruct((rows, width), WIDE)
    counts = ((4,), *[(n, PARTS) for n in (nq, nq, nk, nk)], *[(n,) for n in (nq, nq, nk, nk, nk, nq, nq, nq)])
    sems = [pltpu.SemaphoreType.DMA(count) for count in counts]
    return tuple(
        pl.pallas_call(
            functools.partial(kernel, nq, nk, nka),
            out_shape=(out, out, out),
            in_specs=[smem, smem, hbm, hbm, hbm, hbm],
            out_specs=(vmem, vmem, vmem),
            scratch_shapes=[
                pltpu.VMEM((nq, 2, rows, width), LOW),
                pltpu.VMEM((nk, 2, rows, width), LOW),
                pltpu.VMEM((2, rows, width), jnp.int32),
                pltpu.VMEM((nq, rows), WIDE),
                pltpu.VMEM((nq, rows), WIDE),
                pltpu.VMEM((nq, rows), WIDE),
                pltpu.VMEM((nq, 2 * nq, rows), WIDE),
                pltpu.VMEM((nq, rows), WIDE),
                pltpu.VMEM((nq, rows), WIDE),
                pltpu.VMEM((nq, rows, width), WIDE),
                pltpu.VMEM((nk, rows, width), WIDE),
                pltpu.VMEM((nk, rows, width), WIDE),
                *[pltpu.VMEM((nk, 2, rows, width), LOW)] * 3,
                *[pltpu.VMEM((nq, rows, width), LOW)] * 3,
                *sems,
            ],
            compiler_params=pltpu.CompilerParams(
                collective_id=0, has_side_effects=True, vmem_limit_bytes=60 << 20
            ),
        )(key_scale.reshape(1), value_scale.reshape(1), queries, out_grad, key_codes, value_codes)
    )


def solution(mesh):
    in_specs = (
        P(("pb", "ka"), "ha"),
        P(("ka", "pb"), "ha"),
        P(("ka", "pb"), "ha"),
        P(),
        P(),
        P(("pb", "ka"), "ha"),
    )
    out_specs = (P(("pb", "ka"), "ha"), P(("ka", "pb"), "ha"), P(("ka", "pb"), "ha"))
    return jax.shard_map(shards, mesh=mesh, in_specs=in_specs, out_specs=out_specs, check_vma=False)
```

```python
import functools
import math

import jax
import jax.numpy as jnp
from jax import lax
from jax.experimental import pallas as pl
from jax.experimental.pallas import tpu as pltpu
from jax.sharding import PartitionSpec as P

MESH = pl.DeviceIdType.MESH
LOW = jnp.bfloat16
PARTS = 4
WIDE = jnp.float32


def flipped(rank, step, count):
    total = 0
    bit = 1
    while bit < count:
        one = (rank // bit) % 2
        two = (step // bit) % 2
        total = total + bit * (one + two - 2 * one * two)
        bit *= 2
    return total


def contract(left, right, dims):
    return lax.dot_general(left, right, ((dims[:1], dims[1:]), ((), ())), preferred_element_type=WIDE)


def kernel(
    nq, nk, nka,
    key_scale, value_scale, q_ref, g_ref, kc_ref, vc_ref,
    dq_ref, dk_ref, dv_ref,
    qd, kv, codes, top, total, dot, stats, lse, delta, acc_q, acc_k, acc_v,
    gk_out, gk_mid, gk_in, gq_out, gq_mid, gq_in,
    load, q_send, q_recv, k_send, k_recv, s_send, s_recv,
    gk_send, gk_mid_recv, gk_recv, gq_send, gq_mid_recv, gq_recv,
):
    rows, width = q_ref.shape
    factor = 1.0 / math.sqrt(width)
    log2e = math.log2(math.e)
    pb, ka = lax.axis_index("pb"), lax.axis_index("ka")
    my_a, my_k = pb // nk, pb % nk
    my_q = my_a * nka + ka

    def q_rank(step):
        return flipped(my_q, step, nq)

    def k_rank(step):
        return flipped(my_k, step, nk)

    def q_peer(rank):
        return {"pb": (rank // nka) * nk + my_k, "ka": rank % nka}

    def k_peer(rank):
        return {"pb": my_a * nk + rank, "ka": ka}

    def span(part):
        return pl.ds(part % 2 * (rows // 2), rows // 2)

    def q_copy(block, part, to, sem):
        b, t, s = q_rank(block), q_rank(to), q_rank(sem)
        return pltpu.make_async_remote_copy(
            qd.at[b, part // 2, span(part)], qd.at[b, part // 2, span(part)],
            q_send.at[s, part], q_recv.at[b, part],
            device_id=q_peer(t), device_id_type=MESH)

    def k_copy(block, part, to, sem):
        b, t, s = k_rank(block), k_rank(to), k_rank(sem)
        return pltpu.make_async_remote_copy(
            kv.at[b, part // 2, span(part)], kv.at[b, part // 2, span(part)],
            k_send.at[s, part], k_recv.at[b, part],
            device_id=k_peer(t), device_id_type=MESH)

    def s_copy(rank, slot):
        return pltpu.make_async_remote_copy(
            stats.at[slot], stats.at[slot], s_send.at[rank], s_recv.at[slot],
            device_id=q_peer(rank), device_id_type=MESH)

    def gk_copy(rank, slot):
        return pltpu.make_async_remote_copy(
            gk_out.at[rank], gk_in.at[slot], gk_send.at[rank], gk_recv.at[slot],
            device_id=k_peer(rank), device_id_type=MESH)

    def gk_mid_copy(rank):
        return pltpu.make_async_remote_copy(
            gk_out.at[rank], gk_mid.at[rank], gk_send.at[rank], gk_mid_recv.at[rank],
            device_id=k_peer(k_rank(1)), device_id_type=MESH)

    def gq_copy(rank, slot):
        return pltpu.make_async_remote_copy(
            gq_out.at[rank], gq_in.at[slot], gq_send.at[rank], gq_recv.at[slot],
            device_id=q_peer(rank), device_id_type=MESH)

    def gq_mid_copy(step, slot):
        return pltpu.make_async_remote_copy(
            gq_out.at[q_rank(step)], gq_mid.at[slot], gq_send.at[q_rank(step)], gq_mid_recv.at[slot],
            device_id=q_peer(q_rank(step - nka)), device_id_type=MESH)

    loads = [
        pltpu.make_async_copy(q_ref, qd.at[my_q, 0], load.at[0]),
        pltpu.make_async_copy(g_ref, qd.at[my_q, 1], load.at[1]),
        pltpu.make_async_copy(kc_ref, codes.at[0], load.at[2]),
        pltpu.make_async_copy(vc_ref, codes.at[1], load.at[3]),
    ]
    for one in loads:
        one.start()
    barrier = pltpu.get_barrier_semaphore()
    for step in range(1, nq):
        pl.semaphore_signal(barrier, inc=1, device_id=q_peer(q_rank(step)), device_id_type=MESH)
    for step in range(1, nk):
        pl.semaphore_signal(barrier, inc=1, device_id=k_peer(k_rank(step)), device_id_type=MESH)
    for one in loads:
        one.wait()
    kv[my_k, 0] = (codes[0].astype(WIDE) * key_scale[0]).astype(LOW)
    kv[my_k, 1] = (codes[1].astype(WIDE) * value_scale[0]).astype(LOW)
    pl.semaphore_wait(barrier, nq + nk - 2)

    for part in range(PARTS):
        q_copy(0, part, nka, nka).start()
        for step in range(2, nk, 2):
            k_copy(0, part, step, step).start()
        k_copy(0, part, 1, 1).start()
        for step in range(1, nka):
            q_copy(0, part, step, step).start()
    top[...] = jnp.full_like(top, -1e30)
    total[...] = jnp.zeros_like(total)
    dot[...] = jnp.zeros_like(dot)
    acc_q[...] = jnp.zeros_like(acc_q)
    acc_k[...] = jnp.zeros_like(acc_k)
    acc_v[...] = jnp.zeros_like(acc_v)

    def first(jj, ii):
        j, i = q_rank(jj), k_rank(ii)
        row = pl.ds(j, 1)
        scores = contract(kv[i, 0], qd[j, 0], (1, 1)) * (factor * log2e)
        d_probs = contract(kv[i, 1], qd[j, 1], (1, 1))
        old_top = top[row, :]
        new_top = jnp.maximum(old_top, jnp.max(scores, axis=0, keepdims=True))
        shifted = jnp.exp2(scores - new_top)
        old = jnp.exp2(old_top - new_top)
        total[row, :] = total[row, :] * old + jnp.sum(shifted, axis=0, keepdims=True)
        dot[row, :] = dot[row, :] * old + jnp.sum(shifted * d_probs, axis=0, keepdims=True)
        top[row, :] = new_top

    def first_over(j_range, i_range):
        if len(j_range) * len(i_range) == 0:
            return

        @pl.loop(0, len(j_range) * len(i_range))
        def _(n):
            first(
                j_range.start + n // len(i_range) * j_range.step,
                i_range.start + n % len(i_range) * i_range.step,
            )

    def forward(part):
        q_copy(nka, part, nka, nka).wait_recv()
        for step in range(1, nka):
            q_copy(nka, part, step, nka + step).start()
        for step in range(2, nk, 2):
            k_copy(step, part, step, step).wait_recv()
            k_copy(step, part, 1, step + 1).start()

    first_over(range(0, 1), range(0, 1))
    forward(0)
    for part in range(PARTS):
        k_copy(1, part, 1, 1).wait_recv()
    first_over(range(0, 1), range(1, 2))
    forward(1)
    for step in range(1, nka):
        for part in range(PARTS):
            q_copy(step, part, step, step).wait_recv()
    first_over(range(1, nka), range(0, 2))
    for part in range(2, PARTS):
        forward(part)
    first_over(range(0, nka + 1), range(2, nk, 2))
    first_over(range(nka, nka + 1), range(0, 2))
    for step in range(3, nk, 2):
        for part in range(PARTS):
            k_copy(step, part, step, step).wait_recv()
    first_over(range(0, nka + 1), range(3, nk, 2))
    for step in range(nka + 1, nq):
        for part in range(PARTS):
            q_copy(step, part, step, step).wait_recv()
    first_over(range(nka + 1, nq), range(0, nk))

    stats[my_q, 0:nq, :] = top[...] + jnp.log2(total[...])
    stats[my_q, nq : 2 * nq, :] = dot[...] / total[...]
    for step in range(1, nq):
        s_copy(q_rank(nq - step), my_q).start()
    for step in range(1, nq):
        other = q_rank(step)
        s_copy(other, other).wait_recv()
    parts = [stats[r, 0:nq, :] for r in range(nq)]
    best = functools.reduce(jnp.maximum, parts)
    weights = [jnp.exp2(part - best) for part in parts]
    whole = sum(weights)
    lse[...] = best + jnp.log2(whole)
    delta[...] = sum(w * stats[r, nq : 2 * nq, :] for r, w in enumerate(weights)) / whole

    def second(jj, ii):
        j, i = q_rank(jj), k_rank(ii)
        keys, queries, grads = kv[i, 0], qd[j, 0], qd[j, 1]
        scores = contract(keys, queries, (1, 1)) * (factor * log2e)
        d_probs = contract(kv[i, 1], grads, (1, 1))
        probs = jnp.exp2(scores - lse[pl.ds(j, 1), :])
        d_scores = (probs * (d_probs - delta[pl.ds(j, 1), :])).astype(LOW)
        acc_v[i] += contract(probs.astype(LOW), grads, (1, 0))
        acc_k[i] += contract(d_scores, queries, (1, 0))
        acc_q[j] += contract(keys, d_scores, (0, 0))

    def pack_keys(i):
        gk_out[i, 0] = (acc_k[i] * factor).astype(LOW)
        gk_out[i, 1] = acc_v[i].astype(LOW)

    def pack_queries(j):
        gq_out[j] = (acc_q[j].T * factor).astype(LOW)

    @pl.loop(0, nk // 2 - 1)
    def _(n):
        ii = nk - 1 - 2 * n

        @pl.loop(0, nq, unroll=2)
        def _(jj):
            second(jj, ii)

        pack_keys(k_rank(ii))
        gk_mid_copy(k_rank(ii)).start()

    @pl.loop(0, nq - nka)
    def _(n):
        jj = nq - 1 - n

        @pl.loop(0, nk // 2 + 1)
        def _(m):
            second(jj, 2 * (m - 1) + 3 * ((nk // 2 + 1 - m) // (nk // 2 + 1)))

        @pl.when(jj > nka)
        def _():
            pack_queries(q_rank(jj))
            gq_mid_copy(jj, my_q).start()

    far = q_rank(nka)
    query_sum = acc_q[far].T * factor
    for step in range(1, nka):
        gq_mid_copy(nka + step, q_rank(step)).wait_recv()
        query_sum = query_sum + gq_mid[q_rank(step)].astype(WIDE)
    gq_out[far] = query_sum.astype(LOW)
    gq_copy(far, my_q).start()

    @pl.loop(0, nk // 2 - 1)
    def _(n):
        i = k_rank(2 + 2 * n)

        @pl.loop(0, nka, unroll=2)
        def _(jj):
            second(jj, 2 + 2 * n)

        gk_mid_copy(i).wait_recv()
        gk_out[i, 0] = (acc_k[i] * factor + gk_mid[i, 0].astype(WIDE)).astype(LOW)
        gk_out[i, 1] = (acc_v[i] + gk_mid[i, 1].astype(WIDE)).astype(LOW)
        gk_copy(i, my_k).start()

    @pl.loop(0, 2 * nka)
    def _(n):
        jj = nka - 1 - n % nka
        second(jj, 1 - n // nka)

        @pl.when(n == nka - 1)
        def _():
            pack_keys(k_rank(1))
            gk_copy(k_rank(1), my_k).start()

        @pl.when((n >= nka) & (jj > 0))
        def _():
            pack_queries(q_rank(jj))
            gq_copy(q_rank(jj), my_q).start()

    query_sum = acc_q[my_q].T * factor
    for step in range(nka, 0, -1):
        other = q_rank(step)
        gq_copy(other, other).wait_recv()
        query_sum = query_sum + gq_in[other].astype(WIDE)
    dq_ref[...] = query_sum
    key_sum, value_sum = acc_k[my_k] * factor, acc_v[my_k]
    for step in (*range(2, nk, 2), 1):
        other = k_rank(step)
        gk_copy(other, other).wait_recv()
        key_sum = key_sum + gk_in[other, 0].astype(WIDE)
        value_sum = value_sum + gk_in[other, 1].astype(WIDE)
    dk_ref[...] = key_sum
    dv_ref[...] = value_sum
    for step in range(1, nq):
        other = q_rank(step)
        for part in range(PARTS):
            q_copy(0, part, step, step).wait_send()
        s_copy(other, my_q).wait_send()
        gq_copy(other, my_q).wait_send()
    for step in range(1, nk):
        other = k_rank(step)
        for part in range(PARTS):
            k_copy(0, part, step, step).wait_send()
        gk_copy(other, my_k).wait_send()


def shards(queries, key_codes, value_codes, key_scale, value_scale, out_grad):
    rows, width = queries.shape
    npb, nka = lax.axis_size("pb"), lax.axis_size("ka")
    nq, nk = 2 * nka, npb // 2
    vmem = pl.BlockSpec(memory_space=pltpu.VMEM)
    hbm = pl.BlockSpec(memory_space=pltpu.HBM)
    smem = pl.BlockSpec(memory_space=pltpu.SMEM)
    out = jax.ShapeDtypeStruct((rows, width), WIDE)
    counts = ((4,), *[(n, PARTS) for n in (nq, nq, nk, nk)], *[(n,) for n in (nq, nq, nk, nk, nk, nq, nq, nq)])
    sems = [pltpu.SemaphoreType.DMA(count) for count in counts]
    return tuple(
        pl.pallas_call(
            functools.partial(kernel, nq, nk, nka),
            out_shape=(out, out, out),
            in_specs=[smem, smem, hbm, hbm, hbm, hbm],
            out_specs=(vmem, vmem, vmem),
            scratch_shapes=[
                pltpu.VMEM((nq, 2, rows, width), LOW),
                pltpu.VMEM((nk, 2, rows, width), LOW),
                pltpu.VMEM((2, rows, width), jnp.int32),
                pltpu.VMEM((nq, rows), WIDE),
                pltpu.VMEM((nq, rows), WIDE),
                pltpu.VMEM((nq, rows), WIDE),
                pltpu.VMEM((nq, 2 * nq, rows), WIDE),
                pltpu.VMEM((nq, rows), WIDE),
                pltpu.VMEM((nq, rows), WIDE),
                pltpu.VMEM((nq, width, rows), WIDE),
                pltpu.VMEM((nk, rows, width), WIDE),
                pltpu.VMEM((nk, rows, width), WIDE),
                *[pltpu.VMEM((nk, 2, rows, width), LOW)] * 3,
                *[pltpu.VMEM((nq, rows, width), LOW)] * 3,
                *sems,
            ],
            compiler_params=pltpu.CompilerParams(
                collective_id=0, has_side_effects=True, vmem_limit_bytes=60 << 20
            ),
        )(key_scale.reshape(1), value_scale.reshape(1), queries, out_grad, key_codes, value_codes)
    )


def solution(mesh):
    in_specs = (
        P(("pb", "ka"), "ha"),
        P(("ka", "pb"), "ha"),
        P(("ka", "pb"), "ha"),
        P(),
        P(),
        P(("pb", "ka"), "ha"),
    )
    out_specs = (P(("pb", "ka"), "ha"), P(("ka", "pb"), "ha"), P(("ka", "pb"), "ha"))
    return jax.shard_map(shards, mesh=mesh, in_specs=in_specs, out_specs=out_specs, check_vma=False)
```
